32 devices in a mesh: prow: 4 (over x, core), pcol: 8 (over z, y).
Axes of the slice: x: 2, y: 2, z: 4, core: 2. Of those that a mesh axis runs over, the one named last changes fastest.
Arguments:
- diag_block: float32 [640, 640], P('prow'), as said below
- panel_below: float32 [18432, 640], P(('prow', 'pcol')), may hold values from -0.5 to 0.5
- trailing: float32 [18432, 18432], P('prow', 'pcol'), may hold values from -6 to 6
Outputs:
- factor_diag: float32 [640, 640], P('prow')
- factor_below: float32 [18432, 640], P(('prow', 'pcol'))
- updated: float32 [18432, 18432], P('prow', 'pcol')
The draws below stay inside these ranges and needn't reach their ends.
Inputs may be any that keep to these rules, and one draw needn't show every extreme that they name: `diag_block`: symmetric and positive definite, its smallest eigenvalue above 0.5.
All inputs are finite; a program needn't handle non-finite values.
Results may differ from the reference program's by a relative error of at most 0.0003.
Values sent between devices are 32-bit elements; how exact they have to be, the bound alone decides.
A program may use at most 192 MiB of HBM per device.

```python
import jax
import jax.numpy as jnp
from jax import lax

M = 18432
P_SIZE = 640


def draw_diag_block(key, part):
    east_key = jax.random.fold_in(key, 11)
    north_key = jax.random.fold_in(key, 23)
    nugget_key = jax.random.fold_in(key, 37)
    length_scale = 1.265 / P_SIZE ** 0.5
    variance = 20.0
    nugget = jax.random.uniform(nugget_key, (P_SIZE,), jnp.float32, 0.6, 1.2)
    eastings = jax.random.uniform(east_key, (P_SIZE,), jnp.float32, 0.0, 1.0)
    northings = jax.random.uniform(north_key, (P_SIZE,), jnp.float32, 0.0, 1.0)
    east_gap = eastings[:, None] - eastings[None, :]
    north_gap = northings[:, None] - northings[None, :]
    distance = jnp.sqrt(east_gap * east_gap + north_gap * north_gap)
    scaled = distance * (3.0 ** 0.5 / length_scale)
    kernel = variance * (1.0 + scaled) * jnp.exp(-scaled)
    return kernel + jnp.diag(nugget)


def steps_of(key, dims, pieces, least, top_value):
    def one(position, blocks):
        heights = jax.random.uniform(jax.random.fold_in(jax.random.fold_in(key, 6), position), (blocks,), jnp.float32, least / len(pieces), top_value / len(pieces))
        return jnp.repeat(jnp.exp(heights), dims[position] // blocks).reshape((-1,) + (1,) * (len(dims) - position - 1))

    loudness = one(*pieces[0])
    for cut in pieces[1:]:
        loudness = loudness * one(*cut)
    return loudness


def bell_draw(stream_key, extent, width, limit, pieces=(), dtype=jnp.bfloat16):
    factor_of = steps_of(stream_key, extent, pieces, -0.22, 0.18) if pieces else 1.0
    result = jax.random.normal(stream_key, extent, jnp.float32) * width * factor_of
    return jnp.minimum(jnp.maximum(result, -limit), limit).astype(dtype)


def setup_inputs(seed: int = 0) -> dict:
    key_of = jax.random.split(jax.random.key(seed), 4)
    return {
        "diag_block": draw_diag_block(jax.random.fold_in(key_of[3], 71), 0),
        "panel_below": bell_draw(key_of[1], (M, P_SIZE), (P_SIZE // 4) ** -0.5, 0.5, ((0, 32),), jnp.float32),
        "trailing": bell_draw(key_of[2], (M, M), 1.0, 6.0, ((0, 4), (1, 8)), jnp.float32),
    }


def reference(diag_block, panel_below, trailing):
    factor_diag = jnp.linalg.cholesky(diag_block)
    factor_below = jax.scipy.linalg.solve_triangular(factor_diag, panel_below.T, lower=True).T
    product = lax.dot_general(factor_below.astype(jnp.float32), factor_below.astype(jnp.float32), (((1,), (1,)), ((), ())), precision=lax.Precision.HIGHEST, preferred_element_type=jnp.float32)
    updated = trailing - product
    return (factor_diag, factor_below, updated)
```

```python
import functools

import jax
import jax.numpy as jnp
import numpy as np
from jax import lax
from jax.experimental import pallas as pl
from jax.experimental.pallas import tpu as pltpu
from jax.sharding import PartitionSpec as P

B = 128
F32 = jnp.float32
BF16 = jnp.bfloat16
VMEM = pl.BlockSpec(memory_space=pltpu.VMEM)


def dot(a, b, contract=((1,), (0,)), precision=lax.Precision.HIGHEST):
    return lax.dot_general(a, b, (contract, ((), ())), precision=precision, preferred_element_type=F32)


def split(x):
    high = x.astype(BF16)
    return high, (x - high.astype(F32)).astype(BF16)


def lanes(x, q):
    return jnp.broadcast_to(x[:, q : q + 1], (8, B))


def sublanes(x, i):
    return jnp.broadcast_to(x[i : i + 1, :], (8, B))


def eliminate(block_ref):
    count = B // 8
    sub = lax.broadcasted_iota(jnp.int32, (8, B), 0)
    lane = lax.broadcasted_iota(jnp.int32, (8, B), 1)
    a = [block_ref[8 * r : 8 * r + 8, :B] for r in range(count)]
    m = [jnp.where(lane == sub + 8 * r, 1.0, 0.0).astype(F32) for r in range(count)]
    upper, inv = [], []
    for g in range(count):
        columns = [lanes(a[g], 8 * g + q) for q in range(8)]
        d = {(i, q): sublanes(columns[q], i) for q in range(8) for i in range(q + 1)}
        ua = [sublanes(a[g], q) for q in range(8)]
        um = [sublanes(m[g], q) for q in range(8)]
        scale = []
        for p in range(8):
            scale.append(lax.rsqrt(d[p, p]))
            for q in range(p + 1, 8):
                d[p, q] = d[p, q] * scale[p]
            ua[p] = ua[p] * scale[p]
            um[p] = um[p] * scale[p]
            for i in range(p + 1, 8):
                for q in range(i, 8):
                    d[i, q] = d[i, q] - d[p, i] * d[p, q]
                ua[i] = ua[i] - d[p, i] * ua[p]
                um[i] = um[i] - d[p, i] * um[p]
        rows_a, rows_m = ua[7], um[7]
        for q in range(7):
            rows_a = jnp.where(sub == q, ua[q], rows_a)
            rows_m = jnp.where(sub == q, um[q], rows_m)
        upper.append(jnp.where(lane >= sub + 8 * g, rows_a, 0.0))
        inv.append(rows_m)
        if g == count - 1:
            break
        for p in range(7, -1, -1):
            ua[p] = ua[p] * scale[p]
            um[p] = um[p] * scale[p]
            for q in range(p):
                ua[q] = ua[q] - d[q, p] * ua[p]
                um[q] = um[q] - d[q, p] * um[p]
        for r in range(g + 1, count):
            column = lanes(a[r], 8 * g)
            sum_a, sum_m = column * ua[0], column * um[0]
            for q in range(1, 8):
                column = lanes(a[r], 8 * g + q)
                sum_a = sum_a + column * ua[q]
                sum_m = sum_m + column * um[q]
            a[r] = a[r] - sum_a
            m[r] = m[r] - sum_m
    return jnp.concatenate(upper, 0), jnp.concatenate(inv, 0)


def step_kernel(k, rest, *refs):
    s_ref = refs[0]
    refs = refs[1:]
    t_ref = None
    if k:
        t_ref, refs = refs[0], refs[1:]
    l_ref, x_ref = refs[0], refs[1]
    upper, inv = eliminate(s_ref)
    l_ref[:B, :] = upper.T
    if k:
        x_ref[:, : B * k] = dot(inv, t_ref[:B, :])
    x_ref[:, B * k :] = inv
    if rest:
        panel = dot(s_ref[B:, :B], inv, ((1,), (1,)))
        l_ref[B:, :] = panel
        s_out, t_out = refs[2], refs[3]
        s_out[...] = s_ref[B:, B:] - dot(panel, panel, ((1,), (1,)))
        if k:
            t_out[:, : B * k] = t_ref[B:, :] - dot(panel, x_ref[:, : B * k])
        t_out[:, B * k :] = -dot(panel, inv)


def finish_kernel(nb, *refs):
    ls, xs, panel_ref = refs[:nb], refs[nb : 2 * nb], refs[2 * nb]
    l_ref, si_ref, f_ref, x_ref = refs[2 * nb + 1 :]
    l_ref[...] = jnp.zeros_like(l_ref)
    x_ref[...] = jnp.zeros_like(x_ref)
    for k in range(nb):
        l_ref[B * k :, B * k : B * k + B] = ls[k][...]
        x_ref[B * k : B * k + B, : B * k + B] = xs[k][...]
    x = x_ref[...]
    f_ref[...] = dot(panel_ref[...], x, ((1,), (1,)))
    si_ref[...] = dot(x, x, ((0,), (0,)))


def cost(flops, size):
    return pl.CostEstimate(flops=int(flops), bytes_accessed=int(size), transcendentals=0)


PARAMS = dict(vmem_limit_bytes=40 << 20)


def factorize(whole_diag, panel):
    size = whole_diag.shape[0]
    nb = size // B
    s, t = whole_diag, None
    ls, xs = [], []
    for k in range(nb):
        n = size - B * k
        rest = n - B
        out = [jax.ShapeDtypeStruct((n, B), F32), jax.ShapeDtypeStruct((B, B * (k + 1)), F32)]
        if rest:
            out += [jax.ShapeDtypeStruct((rest, rest), F32), jax.ShapeDtypeStruct((rest, B * (k + 1)), F32)]
        args = [s] + ([t] if k else [])
        res = pl.pallas_call(
            functools.partial(step_kernel, k, rest),
            out_shape=out,
            in_specs=[VMEM] * len(args),
            out_specs=[VMEM] * len(out),
            compiler_params=pltpu.CompilerParams(**PARAMS),
            cost_estimate=cost(14e9, 4 * n * n),
            name="diag_step",
        )(*args)
        ls.append(res[0])
        xs.append(res[1])
        if rest:
            s, t = res[2], res[3]
    return pl.pallas_call(
        functools.partial(finish_kernel, nb),
        out_shape=[
            jax.ShapeDtypeStruct((size, size), F32),
            jax.ShapeDtypeStruct((size, size), F32),
            jax.ShapeDtypeStruct(panel.shape, F32),
        ],
        in_specs=[VMEM] * (2 * nb + 1),
        out_specs=[VMEM] * 3,
        scratch_shapes=[pltpu.VMEM((size, size), F32)],
        compiler_params=pltpu.CompilerParams(**PARAMS),
        cost_estimate=cost(8e9, 4 * 5 * size * size),
        name="diag_finish",
    )(*ls, *xs, panel)


def update_kernel(si_ref, col_ref, row_ref, t_ref, o_ref, w_ref):
    k = si_ref.shape[0]

    @pl.when(pl.program_id(0) == 0)
    def _():
        high, low = split(si_ref[...])
        left = jnp.concatenate([high, high, low], 1)
        width = w_ref.shape[1]
        tile = 256 if width % 256 == 0 else width
        for c in range(0, width, tile):
            bh, bl = split(col_ref[c : c + tile, :])
            right = jnp.concatenate([bh, bl, bh], 1)
            w = dot(left, right, ((1,), (1,)), lax.Precision.DEFAULT)
            wh, wl = split(w)
            w_ref[:k, c : c + tile] = wh
            w_ref[k : 2 * k, c : c + tile] = wl
            w_ref[2 * k :, c : c + tile] = wh

    high, low = split(row_ref[...])
    a = jnp.concatenate([high, high, low], 1)
    o_ref[...] = t_ref[...] - dot(a, w_ref[...], precision=lax.Precision.DEFAULT)


def update(inverse, columns, rows, trailing):
    m, n = trailing.shape
    k = inverse.shape[0]
    tm = 256
    return pl.pallas_call(
        update_kernel,
        grid=(m // tm,),
        out_shape=jax.ShapeDtypeStruct((m, n), F32),
        in_specs=[
            VMEM,
            VMEM,
            pl.BlockSpec((tm, k), lambda i: (i, 0)),
            pl.BlockSpec((tm, n), lambda i: (i, 0)),
        ],
        out_specs=pl.BlockSpec((tm, n), lambda i: (i, 0)),
        scratch_shapes=[pltpu.VMEM((3 * k, n), BF16)],
        compiler_params=pltpu.CompilerParams(vmem_limit_bytes=58 << 20),
        cost_estimate=cost(6 * m * n * k, 8 * m * n),
        name="trailing_update",
    )(inverse, columns, rows, trailing)


def gather_diag(diag_block, n_row):
    rows = diag_block.shape[0]
    me = lax.axis_index("prow")
    whole = jnp.zeros((rows * n_row, diag_block.shape[1]), F32)
    whole = lax.dynamic_update_slice_in_dim(whole, diag_block, me * rows, 0)
    for d in range(1, n_row):
        got = lax.ppermute(diag_block, "prow", [(i, (i + d) % n_row) for i in range(n_row)])
        whole = lax.dynamic_update_slice_in_dim(whole, got, (me + n_row - d) % n_row * rows, 0)
    return whole


ORDER = (0, 2, 4, 6, 7, 5, 3, 1)


def gather_ring(panel, n_row, n_col):
    rows, width = panel.shape
    me, mine = lax.axis_index("prow"), lax.axis_index("pcol")
    place = {c: i for i, c in enumerate(ORDER)}
    right = [(ORDER[i], ORDER[(i + 1) % n_col]) for i in range(n_col)]
    left = [(b, a) for a, b in right]
    at = lambda o: jnp.asarray([ORDER[(place[c] + o) % n_col] for c in range(n_col)], jnp.int32)[mine]

    def put(buf, value, o, start=0):
        return lax.dynamic_update_slice_in_dim(buf, value, at(o) * rows + start, 0)

    owner_of = [c * n_row // n_col for c in range(n_col)]
    owner = mine * n_row // n_col
    need = []
    for c in range(n_col):
        first = c * n_row % n_col
        wanted = list(range(first, first + n_row))
        far = lambda w: min((place[w] - place[c]) % n_col, (place[c] - place[w]) % n_col)
        need.append(sorted(wanted, key=far))
    need = jnp.asarray(need, jnp.int32)
    axes = ("prow", "pcol")
    across = [(owner_of[c] * n_col + c, (owner_of[c] ^ 2) * n_col + c) for c in range(n_col)]
    beside = [(o * n_col + c, (o ^ 1) * n_col + c) for c in range(n_col) for o in (owner_of[c], owner_of[c] ^ 2)]
    column = jnp.zeros((rows * n_row, width), F32)

    def send_column(column, buf, slot):
        which = need[mine, slot]
        block = lax.dynamic_slice_in_dim(buf, which * rows, rows, 0)
        got = lax.ppermute(block, axes, across)
        block = jnp.where(me == owner, block, got)
        got = lax.ppermute(block, axes, beside)
        block = jnp.where((me == owner) | (me == (owner ^ 2)), block, got)
        return lax.dynamic_update_slice_in_dim(column, block, which % n_row * rows, 0)

    buf = jnp.zeros((rows * n_col, width), F32)
    buf = put(buf, panel, 0)
    from_left = from_right = panel
    for s in (1, 2, 3):
        from_left = lax.ppermute(from_left, "pcol", right)
        from_right = lax.ppermute(from_right, "pcol", left)
        buf = put(buf, from_left, -s)
        buf = put(buf, from_right, s)
        if s == 2:
            column = send_column(column, buf, 0)
        if s == 3:
            column = send_column(column, buf, 1)
            column = send_column(column, buf, 2)
    half = rows // 2
    low = lax.ppermute(from_left[:half], "pcol", right)
    high = lax.ppermute(from_right[half:], "pcol", left)
    buf = put(buf, low, 4)
    buf = put(buf, high, 4, half)
    column = send_column(column, buf, 3)
    return buf, column


def gather_plain(panel, n_row, n_col):
    rows = panel.shape[0]
    me, mine = lax.axis_index("prow"), lax.axis_index("pcol")
    row_panel = lax.all_gather(panel, "pcol", axis=0, tiled=True)
    owner = mine * n_row // n_col
    start = mine * n_row * rows - owner * n_col * rows
    block = lax.dynamic_slice_in_dim(row_panel, start, n_row * rows, 0)
    return row_panel, lax.psum(jnp.where(me == owner, block, 0.0), "prow")


def local(n_row, n_col, diag_block, panel_below, trailing):
    whole_diag = gather_diag(diag_block, n_row)
    gather = gather_ring if (n_row, n_col) == (4, 8) else gather_plain
    rows, columns = gather(panel_below, n_row, n_col)
    factor, inverse, own = factorize(whole_diag, panel_below)
    diag_rows = diag_block.shape[0]
    factor_diag = lax.dynamic_slice_in_dim(factor, lax.axis_index("prow") * diag_rows, diag_rows, 0)
    return factor_diag, own, update(inverse, columns, rows, trailing)


def solution(mesh):
    return jax.shard_map(
        functools.partial(local, mesh.shape["prow"], mesh.shape["pcol"]),
        mesh=mesh,
        in_specs=(P("prow", None), P(("prow", "pcol"), None), P("prow", "pcol")),
        out_specs=(P("prow", None), P(("prow", "pcol"), None), P("prow", "pcol")),
        check_vma=False,
    )
```

```python
import functools
import random

import jax
import jax.numpy as jnp
import numpy as np
from jax import lax
from jax.experimental import pallas as pl
from jax.experimental.pallas import tpu as pltpu
from jax.sharding import PartitionSpec as P

B = 128
F32 = jnp.float32
BF16 = jnp.bfloat16
VMEM = pl.BlockSpec(memory_space=pltpu.VMEM)


def dot(a, b, contract=((1,), (0,)), precision=lax.Precision.HIGHEST):
    return lax.dot_general(a, b, (contract, ((), ())), precision=precision, preferred_element_type=F32)


def split(x):
    high = x.astype(BF16)
    return high, (x - high.astype(F32)).astype(BF16)


def lanes(x, q):
    return jnp.broadcast_to(x[:, q : q + 1], (8, B))


def sublanes(x, i):
    return jnp.broadcast_to(x[i : i + 1, :], (8, B))


def eliminate(block_ref):
    count = B // 8
    sub = lax.broadcasted_iota(jnp.int32, (8, B), 0)
    lane = lax.broadcasted_iota(jnp.int32, (8, B), 1)
    a = [block_ref[8 * r : 8 * r + 8, :B] for r in range(count)]
    m = [jnp.where(lane == sub + 8 * r, 1.0, 0.0).astype(F32) for r in range(count)]
    upper, inv = [], []
    for g in range(count):
        columns = [lanes(a[g], 8 * g + q) for q in range(8)]
        d = {(i, q): sublanes(columns[q], i) for q in range(8) for i in range(q + 1)}
        ua = [sublanes(a[g], q) for q in range(8)]
        um = [sublanes(m[g], q) for q in range(8)]
        scale = []
        for p in range(8):
            scale.append(lax.rsqrt(d[p, p]))
            for q in range(p + 1, 8):
                d[p, q] = d[p, q] * scale[p]
            ua[p] = ua[p] * scale[p]
            um[p] = um[p] * scale[p]
            for i in range(p + 1, 8):
                for q in range(i, 8):
                    d[i, q] = d[i, q] - d[p, i] * d[p, q]
                ua[i] = ua[i] - d[p, i] * ua[p]
                um[i] = um[i] - d[p, i] * um[p]
        rows_a, rows_m = ua[7], um[7]
        for q in range(7):
            rows_a = jnp.where(sub == q, ua[q], rows_a)
            rows_m = jnp.where(sub == q, um[q], rows_m)
        upper.append(jnp.where(lane >= sub + 8 * g, rows_a, 0.0))
        inv.append(rows_m)
        if g == count - 1:
            break
        for p in range(7, -1, -1):
            ua[p] = ua[p] * scale[p]
            um[p] = um[p] * scale[p]
            for q in range(p):
                ua[q] = ua[q] - d[q, p] * ua[p]
                um[q] = um[q] - d[q, p] * um[p]
        for r in range(g + 1, count):
            column = lanes(a[r], 8 * g)
            sum_a, sum_m = column * ua[0], column * um[0]
            for q in range(1, 8):
                column = lanes(a[r], 8 * g + q)
                sum_a = sum_a + column * ua[q]
                sum_m = sum_m + column * um[q]
            a[r] = a[r] - sum_a
            m[r] = m[r] - sum_m
    return jnp.concatenate(upper, 0), jnp.concatenate(inv, 0)


def step_kernel(k, rest, *refs):
    s_ref = refs[0]
    refs = refs[1:]
    t_ref = None
    if k:
        t_ref, refs = refs[0], refs[1:]
    l_ref, x_ref = refs[0], refs[1]
    upper, inv = eliminate(s_ref)
    l_ref[:B, :] = upper.T
    if k:
        x_ref[:, : B * k] = dot(inv, t_ref[:B, :])
    x_ref[:, B * k :] = inv
    if rest:
        panel = dot(s_ref[B:, :B], inv, ((1,), (1,)))
        l_ref[B:, :] = panel
        s_out, t_out = refs[2], refs[3]
        s_out[...] = s_ref[B:, B:] - dot(panel, panel, ((1,), (1,)))
        if k:
            t_out[:, : B * k] = t_ref[B:, :] - dot(panel, x_ref[:, : B * k])
        t_out[:, B * k :] = -dot(panel, inv)


def finish_kernel(nb, *refs):
    ls, xs, panel_ref = refs[:nb], refs[nb : 2 * nb], refs[2 * nb]
    l_ref, si_ref, f_ref, x_ref = refs[2 * nb + 1 :]
    l_ref[...] = jnp.zeros_like(l_ref)
    x_ref[...] = jnp.zeros_like(x_ref)
    for k in range(nb):
        l_ref[B * k :, B * k : B * k + B] = ls[k][...]
        x_ref[B * k : B * k + B, : B * k + B] = xs[k][...]
    x = x_ref[...]
    f_ref[...] = dot(panel_ref[...], x, ((1,), (1,)))
    si_ref[...] = dot(x, x, ((0,), (0,)))


def cost(flops, size):
    return pl.CostEstimate(flops=int(flops), bytes_accessed=int(size), transcendentals=0)


PARAMS = dict(vmem_limit_bytes=40 << 20)


def factorize(whole_diag, panel):
    size = whole_diag.shape[0]
    nb = size // B
    s, t = whole_diag, None
    ls, xs = [], []
    for k in range(nb):
        n = size - B * k
        rest = n - B
        out = [jax.ShapeDtypeStruct((n, B), F32), jax.ShapeDtypeStruct((B, B * (k + 1)), F32)]
        if rest:
            out += [jax.ShapeDtypeStruct((rest, rest), F32), jax.ShapeDtypeStruct((rest, B * (k + 1)), F32)]
        args = [s] + ([t] if k else [])
        res = pl.pallas_call(
            functools.partial(step_kernel, k, rest),
            out_shape=out,
            in_specs=[VMEM] * len(args),
            out_specs=[VMEM] * len(out),
            compiler_params=pltpu.CompilerParams(**PARAMS),
            cost_estimate=cost(14e9, 4 * n * n),
            name="diag_step",
        )(*args)
        ls.append(res[0])
        xs.append(res[1])
        if rest:
            s, t = res[2], res[3]
    return pl.pallas_call(
        functools.partial(finish_kernel, nb),
        out_shape=[
            jax.ShapeDtypeStruct((size, size), F32),
            jax.ShapeDtypeStruct((size, size), F32),
            jax.ShapeDtypeStruct(panel.shape, F32),
        ],
        in_specs=[VMEM] * (2 * nb + 1),
        out_specs=[VMEM] * 3,
        scratch_shapes=[pltpu.VMEM((size, size), F32)],
        compiler_params=pltpu.CompilerParams(**PARAMS),
        cost_estimate=cost(8e9, 4 * 5 * size * size),
        name="diag_finish",
    )(*ls, *xs, panel)


def update_kernel(where_ref, si_ref, col_ref, row_ref, t_ref, o_ref, w_ref):
    k = si_ref.shape[0]

    @pl.when(pl.program_id(0) == 0)
    def _():
        high, low = split(si_ref[...])
        left = jnp.concatenate([high, high, low], 1)
        width = w_ref.shape[1]
        tile = 256 if width % 256 == 0 else width
        for c in range(0, width, tile):
            bh, bl = split(col_ref[c : c + tile, :])
            right = jnp.concatenate([bh, bl, bh], 1)
            w = dot(left, right, ((1,), (1,)), lax.Precision.DEFAULT)
            wh, wl = split(w)
            w_ref[:k, c : c + tile] = wh
            w_ref[k : 2 * k, c : c + tile] = wl
            w_ref[2 * k :, c : c + tile] = wh

    high, low = split(row_ref[...])
    a = jnp.concatenate([high, high, low], 1)
    o_ref[...] = t_ref[...] - dot(a, w_ref[...], precision=lax.Precision.DEFAULT)


def update(inverse, columns, rows, trailing, where=None):
    m, n = trailing.shape
    k = inverse.shape[0]
    tm = next(s for s in (384, 256, 128, 64, 32, 16, 8) if m % s == 0)
    where = jnp.zeros((1,), jnp.int32) if where is None else where.reshape((1,))
    return pl.pallas_call(
        update_kernel,
        grid_spec=pltpu.PrefetchScalarGridSpec(
            num_scalar_prefetch=1,
            grid=(m // tm,),
            in_specs=[
                pl.BlockSpec((k, k), lambda i, w: (0, 0)),
                pl.BlockSpec((n, k), lambda i, w: (w[0], 0), pipeline_mode=pl.Buffered(1)),
                pl.BlockSpec((tm, k), lambda i, w: (i, 0)),
                pl.BlockSpec((tm, n), lambda i, w: (i, 0)),
            ],
            out_specs=pl.BlockSpec((tm, n), lambda i, w: (i, 0)),
            scratch_shapes=[pltpu.VMEM((3 * k, n), BF16)],
        ),
        out_shape=jax.ShapeDtypeStruct((m, n), F32),
        compiler_params=pltpu.CompilerParams(vmem_limit_bytes=58 << 20),
        cost_estimate=cost(6 * m * n * k, 8 * m * n),
        name="trailing_update",
    )(where, inverse, columns, rows, trailing)


def gather_diag(diag_block, n_row):
    rows = diag_block.shape[0]
    me = lax.axis_index("prow")
    whole = jnp.zeros((rows * n_row, diag_block.shape[1]), F32)
    whole = lax.dynamic_update_slice_in_dim(whole, diag_block, me * rows, 0)
    for d in range(1, n_row):
        got = lax.ppermute(diag_block, "prow", [(i, (i + d) % n_row) for i in range(n_row)])
        whole = lax.dynamic_update_slice_in_dim(whole, got, (me + n_row - d) % n_row * rows, 0)
    return whole


HALVES = 2
LAG = 2
NONE = 31


def peer_of(device, way):
    r, c = device
    if way == 0:
        return (r, c - 2) if c >= 2 else None
    if way == 1:
        return (r, c + 2) if c < 6 else None
    return ((r, c ^ 1), (r ^ 2, c), (r ^ 1, c))[way - 2]


def make_plan(seed):
    draw = random.Random(seed)
    devices = [(r, c) for r in range(4) for c in range(8)]
    column_of = lambda b: 2 * b[0] + b[1] // 4
    far = lambda d, e: abs(d[1] // 2 - e[1] // 2) + abs(d[1] % 2 - e[1] % 2)
    every = [(r, c, h) for r in range(4) for c in range(8) for h in range(HALVES)]
    need = {d: {b for b in every if b[0] == d[0] or column_of(b) == d[1]} for d in devices}
    got = {d: {(*d, h): 0 for h in range(HALVES)} for d in devices}
    plan = []
    while not all(need[d] <= set(got[d]) for d in devices):
        t, slot = len(plan), {}

        def choose(senders, way, score):
            best = None
            for d in senders:
                e = peer_of(d, way)
                for b, ready in got[d].items():
                    if e is None or ready > t or b in got[e] or b not in need[e]:
                        continue
                    s = score(d, e, b, ready)
                    if s is not None and (best is None or s > best[0]):
                        best = s, d, e, b
            if best:
                slot[best[1], way] = best[3]
                got[best[2]][best[3]] = t + LAG

        def row_score(d, e, b, ready):
            home = (b[0], column_of(b))
            urgent = home[1] // 2 == b[0] and b not in got[home] and far(e, home) < far(d, home)
            lack = sum(b not in got[b[0], o] for o in range(8))
            return urgent, far(d, home) if urgent else lack, draw.random()

        def column_score(d, e, b, ready):
            return (-ready, draw.random()) if column_of(b) == d[1] and e[0] != b[0] else None

        links = [(x, c, way) for x in range(2) for c in range(8) for way in range(3)]
        draw.shuffle(links)
        for x, c, way in links:
            choose([(2 * x, c), (2 * x + 1, c)], way, row_score)
        for x in range(2):
            for c in range(8):
                choose([(2 * x, c), (2 * x + 1, c)], 3, lambda d, e, b, ready: column_score(d, e, b, ready) if b[0] == d[0] else None)
        for d in devices:
            choose([d], 4, column_score)
        plan.append(slot)
    return plan


def place_of(device, b):
    r, c, h = b
    return c * HALVES + h if r == device[0] else 8 * HALVES + c % 4 * HALVES + h


def tables(plan):
    out = []
    for slot in plan:
        ways = []
        for way in range(5):
            send, receive = {}, {}
            for (d, w), b in slot.items():
                if w == way:
                    e = peer_of(d, way)
                    send[d] = receive[e] = place_of(e, b)
            ways.append((send, receive))
        out.append(ways)
    return out


def exchange_kernel(table, diag_ref, panel_ref, buf, l_own, f_ref, si_ref, s_ref, l_ref, x_ref, send_sem, recv_sem, own_sem, diag_send, diag_recv):
    slots = len(table)
    me, mine = lax.axis_index("prow"), lax.axis_index("pcol")
    z, y = lax.div(mine, 2), lax.rem(mine, 2)
    size = s_ref.shape[0]
    part = diag_ref.shape[0]
    half = buf.shape[1]
    other = lax.rem(me + 2, 4)
    sibling = me + 1 - 2 * lax.rem(me, 2)
    peers = [(me, mine - 2), (me, mine + 2), (me, mine + 1 - 2 * y), (other, mine), (sibling, mine)]
    mesh_id = pl.DeviceIdType.MESH

    barrier = pltpu.get_barrier_semaphore()

    @pl.when(z > 0)
    def _():
        pl.semaphore_signal(barrier, inc=1, device_id=(me, mine - 2), device_id_type=mesh_id)

    @pl.when(z < 3)
    def _():
        pl.semaphore_signal(barrier, inc=1, device_id=(me, mine + 2), device_id_type=mesh_id)

    pl.semaphore_signal(barrier, inc=1, device_id=peers[2], device_id_type=mesh_id)
    for d in range(1, 4):
        pl.semaphore_signal(barrier, inc=1, device_id=(lax.rem(me + d, 4), mine), device_id_type=mesh_id)
    own = [
        pltpu.make_async_copy(panel_ref.at[pl.ds(h * half, half)], buf.at[mine * HALVES + h], own_sem.at[h])
        for h in range(HALVES)
    ]
    for c in own:
        c.start()
    my_rows = pl.ds(pl.multiple_of(me * part, 8), part)
    s_ref[my_rows, :] = diag_ref[...]
    for c in own:
        c.wait()
    pl.semaphore_wait(barrier, 4 + jnp.where(z > 0, 1, 0) + jnp.where(z < 3, 1, 0))

    copies = []
    for d in range(1, 4):
        copies.append(
            pltpu.make_async_remote_copy(
                src_ref=s_ref.at[my_rows],
                dst_ref=s_ref.at[my_rows],
                send_sem=diag_send.at[d - 1],
                recv_sem=diag_recv.at[d - 1],
                device_id=(lax.rem(me + d, 4), mine),
                device_id_type=mesh_id,
            )
        )
        copies[-1].start()

    def pick(values):
        packed = [sum(values.get((r, c), NONE) * 32**r for r in range(4)) for c in range(8)]
        got = jnp.int32(packed[7])
        for c in range(7):
            got = jnp.where(mine == c, packed[c], got)
        return got

    def digit(packed):
        got = lax.rem(packed, 32)
        for r in range(1, 4):
            got = jnp.where(me == r, lax.rem(lax.div(packed, 32**r), 32), got)
        return got

    def look(t, way, side):
        if isinstance(t, int):
            values = table[t][way][side]
            return digit(pick(values)) if values else None
        got = pick(table[0][way][side])
        for i in range(1, min(slots, size // B + 1)):
            got = jnp.where(t == i, pick(table[i][way][side]), got)
        return digit(got)

    def copy(way, parity, place):
        if way >= 3:
            src = jnp.where(me == z, place - 8 * HALVES + 4 * HALVES * y, place)
        else:
            src = place
        return pltpu.make_async_remote_copy(
            src_ref=buf.at[src],
            dst_ref=buf.at[place],
            send_sem=send_sem.at[parity, way],
            recv_sem=recv_sem.at[place],
            device_id=peers[way],
            device_id_type=mesh_id,
        )

    def tick(t, before):
        parity = t % 2 if isinstance(t, int) else lax.rem(t, 2)
        now = []
        for way in range(5):
            if isinstance(t, int) and t >= slots:
                now.append((None, None))
                continue
            send, receive = look(t, way, 0), look(t, way, 1)
            if send is not None:

                @pl.when(send < NONE)
                def _(way=way, send=send):
                    copy(way, parity, send).start()

            now.append((send, receive))
        for way in range(5):
            send, receive = before[way] if before else (None, None)
            if receive is not None:

                @pl.when(receive < NONE)
                def _(way=way, receive=receive):
                    copy(way, 1 - parity, receive).wait_recv()

            if send is not None:

                @pl.when(send < NONE)
                def _(way=way, send=send):
                    copy(way, 1 - parity, send).wait_send()

        return now

    before = tick(0, None)
    row = lax.broadcasted_iota(jnp.int32, (size, size), 0)
    lane = lax.broadcasted_iota(jnp.int32, (size, size), 1)
    x_ref[...] = jnp.where(row == lane, 1.0, 0.0).astype(F32)
    for c in copies:
        c.wait()

    def block(b, carry):
        o = pl.multiple_of(b * B, B)
        here = pl.ds(o, B)
        before = [(carry[2 * w], carry[2 * w + 1]) for w in range(5)]
        before = tick(b + 1, before)
        upper, inv = eliminate(s_ref.at[here, here])
        below = lax.broadcasted_iota(jnp.int32, (size, B), 0) >= o + B
        panel = jnp.where(below, dot(s_ref[:, here], inv, ((1,), (1,))), 0.0)
        l_ref[:, here] = panel
        l_ref[here, here] = upper.T
        x = dot(inv, x_ref[here, :])
        s_ref[...] = s_ref[...] - dot(panel, panel, ((1,), (1,)))
        x_ref[...] = x_ref[...] - dot(panel, x)
        x_ref[here, :] = x
        return tuple(v for pair in before for v in pair)

    none = jnp.int32(NONE)
    carry = tuple(none if v is None else v for pair in before for v in pair)
    carry = lax.fori_loop(0, size // B, block, carry)
    before = [(carry[2 * w], carry[2 * w + 1]) for w in range(5)]
    t = size // B + 1
    before = tick(t, before)
    l_own[...] = l_ref[my_rows, :]
    x = x_ref[...]
    f_ref[...] = dot(panel_ref[...], x, ((1,), (1,)))
    before = tick(t + 1, before)
    si_ref[...] = dot(x, x, ((0,), (0,)))
    for i in range(t + 2, slots + 1):
        before = tick(i, before)


def exchange(diag_block, panel, n_col):
    size = diag_block.shape[1]
    rows = panel.shape[0]
    table = tables(make_plan(2))
    slots = len(table)
    places = (n_col + n_col // 2) * HALVES
    dma = pltpu.SemaphoreType.DMA
    return pl.pallas_call(
        functools.partial(exchange_kernel, table),
        out_shape=[
            jax.ShapeDtypeStruct((places, rows // HALVES, size), F32),
            jax.ShapeDtypeStruct(diag_block.shape, F32),
            jax.ShapeDtypeStruct(panel.shape, F32),
            jax.ShapeDtypeStruct((size, size), F32),
        ],
        in_specs=[VMEM, VMEM],
        out_specs=[pl.BlockSpec(memory_space=pl.ANY), VMEM, VMEM, VMEM],
        scratch_shapes=[pltpu.VMEM((size, size), F32)] * 3
        + [dma((2, 5)), dma((places,)), dma((HALVES,)), dma((3,)), dma((3,))],
        compiler_params=pltpu.CompilerParams(collective_id=0, has_side_effects=True, vmem_limit_bytes=50 << 20),
        cost_estimate=cost(14e9, 4 * rows * size * 12),
        name="exchange",
    )(diag_block, panel)


def gather_plain(panel, n_row, n_col):
    rows = panel.shape[0]
    me, mine = lax.axis_index("prow"), lax.axis_index("pcol")
    row_panel = lax.all_gather(panel, "pcol", axis=0, tiled=True)
    owner = mine * n_row // n_col
    start = mine * n_row * rows - owner * n_col * rows
    block = lax.dynamic_slice_in_dim(row_panel, start, n_row * rows, 0)
    return row_panel, lax.psum(jnp.where(me == owner, block, 0.0), "prow")


def local(n_row, n_col, diag_block, panel_below, trailing):
    if (n_row, n_col) == (4, 8):
        buf, factor_diag, own, inverse = exchange(diag_block, panel_below, n_col)
        blocks = buf.reshape((-1, buf.shape[2]))
        z, y = lax.axis_index("pcol") // 2, lax.axis_index("pcol") % 2
        where = jnp.where(lax.axis_index("prow") == z, y, 2).astype(jnp.int32)
        return factor_diag, own, update(inverse, blocks, blocks, trailing, where)
    whole_diag = gather_diag(diag_block, n_row)
    rows, columns = gather_plain(panel_below, n_row, n_col)
    factor, inverse, own = factorize(whole_diag, panel_below)
    diag_rows = diag_block.shape[0]
    factor_diag = lax.dynamic_slice_in_dim(factor, lax.axis_index("prow") * diag_rows, diag_rows, 0)
    return factor_diag, own, update(inverse, columns, rows, trailing)


def solution(mesh):
    return jax.shard_map(
        functools.partial(local, mesh.shape["prow"], mesh.shape["pcol"]),
        mesh=mesh,
        in_specs=(P("prow", None), P(("prow", "pcol"), None), P("prow", "pcol")),
        out_specs=(P("prow", None), P(("prow", "pcol"), None), P("prow", "pcol")),
        check_vma=False,
    )
```

```python
import functools
import random

import jax
import jax.numpy as jnp
import numpy as np
from jax import lax
from jax.experimental import pallas as pl
from jax.experimental.pallas import tpu as pltpu
from jax.sharding import PartitionSpec as P

B = 128
F32 = jnp.float32
BF16 = jnp.bfloat16
VMEM = pl.BlockSpec(memory_space=pltpu.VMEM)


def dot(a, b, contract=((1,), (0,)), precision=lax.Precision.HIGHEST):
    return lax.dot_general(a, b, (contract, ((), ())), precision=precision, preferred_element_type=F32)


def split(x):
    high = x.astype(BF16)
    return high, (x - high.astype(F32)).astype(BF16)


def lanes(x, q):
    return jnp.broadcast_to(x[:, q : q + 1], (8, B))


def sublanes(x, i):
    return jnp.broadcast_to(x[i : i + 1, :], (8, B))


def eliminate(block_ref):
    count = B // 8
    sub = lax.broadcasted_iota(jnp.int32, (8, B), 0)
    lane = lax.broadcasted_iota(jnp.int32, (8, B), 1)
    a = [block_ref[8 * r : 8 * r + 8, :B] for r in range(count)]
    m = [jnp.where(lane == sub + 8 * r, 1.0, 0.0).astype(F32) for r in range(count)]
    upper, inv = [], []
    for g in range(count):
        columns = [lanes(a[g], 8 * g + q) for q in range(8)]
        d = {(i, q): sublanes(columns[q], i) for q in range(8) for i in range(q + 1)}
        ua = [sublanes(a[g], q) for q in range(8)]
        um = [sublanes(m[g], q) for q in range(8)]
        scale = []
        for p in range(8):
            scale.append(lax.rsqrt(d[p, p]))
            for q in range(p + 1, 8):
                d[p, q] = d[p, q] * scale[p]
            ua[p] = ua[p] * scale[p]
            um[p] = um[p] * scale[p]
            for i in range(p + 1, 8):
                for q in range(i, 8):
                    d[i, q] = d[i, q] - d[p, i] * d[p, q]
                ua[i] = ua[i] - d[p, i] * ua[p]
                um[i] = um[i] - d[p, i] * um[p]
        rows_a, rows_m = ua[7], um[7]
        for q in range(7):
            rows_a = jnp.where(sub == q, ua[q], rows_a)
            rows_m = jnp.where(sub == q, um[q], rows_m)
        upper.append(jnp.where(lane >= sub + 8 * g, rows_a, 0.0))
        inv.append(rows_m)
        if g == count - 1:
            break
        for p in range(7, -1, -1):
            ua[p] = ua[p] * scale[p]
            um[p] = um[p] * scale[p]
            for q in range(p):
                ua[q] = ua[q] - d[q, p] * ua[p]
                um[q] = um[q] - d[q, p] * um[p]
        for r in range(g + 1, count):
            column = lanes(a[r], 8 * g)
            sum_a, sum_m = column * ua[0], column * um[0]
            for q in range(1, 8):
                column = lanes(a[r], 8 * g + q)
                sum_a = sum_a + column * ua[q]
                sum_m = sum_m + column * um[q]
            a[r] = a[r] - sum_a
            m[r] = m[r] - sum_m
    return jnp.concatenate(upper, 0), jnp.concatenate(inv, 0)


def step_kernel(k, rest, *refs):
    s_ref = refs[0]
    refs = refs[1:]
    t_ref = None
    if k:
        t_ref, refs = refs[0], refs[1:]
    l_ref, x_ref = refs[0], refs[1]
    upper, inv = eliminate(s_ref)
    l_ref[:B, :] = upper.T
    if k:
        x_ref[:, : B * k] = dot(inv, t_ref[:B, :])
    x_ref[:, B * k :] = inv
    if rest:
        panel = dot(s_ref[B:, :B], inv, ((1,), (1,)))
        l_ref[B:, :] = panel
        s_out, t_out = refs[2], refs[3]
        s_out[...] = s_ref[B:, B:] - dot(panel, panel, ((1,), (1,)))
        if k:
            t_out[:, : B * k] = t_ref[B:, :] - dot(panel, x_ref[:, : B * k])
        t_out[:, B * k :] = -dot(panel, inv)


def finish_kernel(nb, *refs):
    ls, xs, panel_ref = refs[:nb], refs[nb : 2 * nb], refs[2 * nb]
    l_ref, si_ref, f_ref, x_ref = refs[2 * nb + 1 :]
    l_ref[...] = jnp.zeros_like(l_ref)
    x_ref[...] = jnp.zeros_like(x_ref)
    for k in range(nb):
        l_ref[B * k :, B * k : B * k + B] = ls[k][...]
        x_ref[B * k : B * k + B, : B * k + B] = xs[k][...]
    x = x_ref[...]
    f_ref[...] = dot(panel_ref[...], x, ((1,), (1,)))
    si_ref[...] = dot(x, x, ((0,), (0,)))


def cost(flops, size):
    return pl.CostEstimate(flops=int(flops), bytes_accessed=int(size), transcendentals=0)


PARAMS = dict(vmem_limit_bytes=40 << 20)


def factorize(whole_diag, panel):
    size = whole_diag.shape[0]
    nb = size // B
    s, t = whole_diag, None
    ls, xs = [], []
    for k in range(nb):
        n = size - B * k
        rest = n - B
        out = [jax.ShapeDtypeStruct((n, B), F32), jax.ShapeDtypeStruct((B, B * (k + 1)), F32)]
        if rest:
            out += [jax.ShapeDtypeStruct((rest, rest), F32), jax.ShapeDtypeStruct((rest, B * (k + 1)), F32)]
        args = [s] + ([t] if k else [])
        res = pl.pallas_call(
            functools.partial(step_kernel, k, rest),
            out_shape=out,
            in_specs=[VMEM] * len(args),
            out_specs=[VMEM] * len(out),
            compiler_params=pltpu.CompilerParams(**PARAMS),
            cost_estimate=cost(14e9, 4 * n * n),
            name="diag_step",
        )(*args)
        ls.append(res[0])
        xs.append(res[1])
        if rest:
            s, t = res[2], res[3]
    return pl.pallas_call(
        functools.partial(finish_kernel, nb),
        out_shape=[
            jax.ShapeDtypeStruct((size, size), F32),
            jax.ShapeDtypeStruct((size, size), F32),
            jax.ShapeDtypeStruct(panel.shape, F32),
        ],
        in_specs=[VMEM] * (2 * nb + 1),
        out_specs=[VMEM] * 3,
        scratch_shapes=[pltpu.VMEM((size, size), F32)],
        compiler_params=pltpu.CompilerParams(**PARAMS),
        cost_estimate=cost(8e9, 4 * 5 * size * size),
        name="diag_finish",
    )(*ls, *xs, panel)


def update_kernel(where_ref, si_ref, col_ref, row_ref, t_ref, o_ref, w_ref):
    k = si_ref.shape[0]

    @pl.when(pl.program_id(0) == 0)
    def _():
        high, low = split(si_ref[...])
        left = jnp.concatenate([high, high, low], 1)
        width = w_ref.shape[1]
        tile = 256 if width % 256 == 0 else width
        for c in range(0, width, tile):
            bh, bl = split(col_ref[c : c + tile, :])
            right = jnp.concatenate([bh, bl, bh], 1)
            w = dot(left, right, ((1,), (1,)), lax.Precision.DEFAULT)
            wh, wl = split(w)
            w_ref[:k, c : c + tile] = wh
            w_ref[k : 2 * k, c : c + tile] = wl
            w_ref[2 * k :, c : c + tile] = wh

    high, low = split(row_ref[...])
    a = jnp.concatenate([high, high, low], 1)
    o_ref[...] = t_ref[...] - dot(a, w_ref[...], precision=lax.Precision.DEFAULT)


def update(inverse, columns, rows, trailing, where=None):
    m, n = trailing.shape
    k = inverse.shape[0]
    tm = next(s for s in (384, 256, 128, 64, 32, 16, 8) if m % s == 0)
    where = jnp.zeros((1,), jnp.int32) if where is None else where.reshape((1,))
    return pl.pallas_call(
        update_kernel,
        grid_spec=pltpu.PrefetchScalarGridSpec(
            num_scalar_prefetch=1,
            grid=(m // tm,),
            in_specs=[
                pl.BlockSpec((k, k), lambda i, w: (0, 0)),
                pl.BlockSpec((n, k), lambda i, w: (w[0], 0), pipeline_mode=pl.Buffered(1)),
                pl.BlockSpec((tm, k), lambda i, w: (i, 0)),
                pl.BlockSpec((tm, n), lambda i, w: (i, 0)),
            ],
            out_specs=pl.BlockSpec((tm, n), lambda i, w: (i, 0)),
            scratch_shapes=[pltpu.VMEM((3 * k, n), BF16)],
        ),
        out_shape=jax.ShapeDtypeStruct((m, n), F32),
        compiler_params=pltpu.CompilerParams(vmem_limit_bytes=58 << 20),
        cost_estimate=cost(6 * m * n * k, 8 * m * n),
        name="trailing_update",
    )(where, inverse, columns, rows, trailing)


def gather_diag(diag_block, n_row):
    rows = diag_block.shape[0]
    me = lax.axis_index("prow")
    whole = jnp.zeros((rows * n_row, diag_block.shape[1]), F32)
    whole = lax.dynamic_update_slice_in_dim(whole, diag_block, me * rows, 0)
    for d in range(1, n_row):
        got = lax.ppermute(diag_block, "prow", [(i, (i + d) % n_row) for i in range(n_row)])
        whole = lax.dynamic_update_slice_in_dim(whole, got, (me + n_row - d) % n_row * rows, 0)
    return whole


PIECES = 4
LAG = 3
DEPTH = 5
SEED = 2
BASE = 64
NONE = BASE - 1
TICKS = 2


def peer_of(device, way):
    r, c = device
    if way == 0:
        return (r, c - 2) if c >= 2 else None
    if way == 1:
        return (r, c + 2) if c < 6 else None
    return ((r, c ^ 1), (r ^ 2, c), (r ^ 1, c))[way - 2]


def make_plan(seed):
    draw = random.Random(seed)
    devices = [(r, c) for r in range(4) for c in range(8)]
    column_of = lambda b: 2 * b[0] + b[1] // 4
    far = lambda d, e: abs(d[1] // 2 - e[1] // 2) + abs(d[1] % 2 - e[1] % 2)
    every = [(r, c, h) for r in range(4) for c in range(8) for h in range(PIECES)]
    need = {d: {b for b in every if b[0] == d[0] or column_of(b) == d[1]} for d in devices}
    got = {d: {(*d, h): 0 for h in range(PIECES)} for d in devices}
    plan = []
    while not all(need[d] <= set(got[d]) for d in devices):
        t, slot = len(plan), {}

        def choose(senders, way, score):
            best = None
            for d in senders:
                e = peer_of(d, way)
                for b, ready in got[d].items():
                    if e is None or ready > t or b in got[e] or b not in need[e]:
                        continue
                    s = score(d, e, b, ready)
                    if s is not None and (best is None or s > best[0]):
                        best = s, d, e, b
            if best:
                slot[best[1], way] = best[3]
                got[best[2]][best[3]] = t + LAG

        def row_score(d, e, b, ready):
            home = (b[0], column_of(b))
            near = min(far((b[0], o), home) for o in range(8) if b in got[b[0], o])
            urgent = b not in got[home] and far(e, home) < far(d, home) == near
            lack = sum(b not in got[b[0], o] for o in range(8))
            return urgent, far(d, home) if urgent else lack, draw.random()

        def column_score(d, e, b, ready):
            return (-ready, draw.random()) if column_of(b) == d[1] and e[0] != b[0] else None

        links = [(x, c, way) for x in range(2) for c in range(8) for way in range(3)]
        draw.shuffle(links)
        for x, c, way in links:
            choose([(2 * x, c), (2 * x + 1, c)], way, row_score)
        for x in range(2):
            for c in range(8):
                choose([(2 * x, c), (2 * x + 1, c)], 3, lambda d, e, b, ready: column_score(d, e, b, ready) if b[0] == d[0] else None)
        for d in devices:
            choose([d], 4, column_score)
        plan.append(slot)
    return plan


def place_of(device, b):
    r, c, h = b
    return c * PIECES + h if r == device[0] else 8 * PIECES + c % 4 * PIECES + h


def tables(plan):
    out, rest = [], {}
    waited = {(r, c): {(r, c, h) for h in range(PIECES)} for r in range(4) for c in range(8)}
    for slot in plan:
        ways = []
        for way in range(5):
            send, first = {}, {}
            for (d, w), b in slot.items():
                if w == way:
                    e = peer_of(d, way)
                    send[d] = place_of(e, b)
                    rest.setdefault(e, []).append(b)
            ways.append((send, first))
        for way in range(5):
            for (d, w), b in slot.items():
                if w == way and b not in waited[d]:
                    ways[way][1][d] = place_of(d, b)
                    waited[d].add(b)
        out.append(ways)
    rest = {d: [place_of(d, b) for b in got if b not in waited[d]] for d, got in rest.items()}
    return out, rest


def exchange_kernel(table, rest, diag_ref, panel_ref, buf, l_own, f_ref, si_ref, s_ref, l_ref, x_ref, send_sem, recv_sem, own_sem, diag_send, diag_recv):
    slots = len(table)
    me, mine = lax.axis_index("prow"), lax.axis_index("pcol")
    z, y = lax.div(mine, 2), lax.rem(mine, 2)
    size = s_ref.shape[0]
    part = diag_ref.shape[0]
    half = buf.shape[1]
    other = lax.rem(me + 2, 4)
    sibling = me + 1 - 2 * lax.rem(me, 2)
    peers = [(me, mine - 2), (me, mine + 2), (me, mine + 1 - 2 * y), (other, mine), (sibling, mine)]
    mesh_id = pl.DeviceIdType.MESH

    barrier = pltpu.get_barrier_semaphore()

    @pl.when(z > 0)
    def _():
        pl.semaphore_signal(barrier, inc=1, device_id=(me, mine - 2), device_id_type=mesh_id)

    @pl.when(z < 3)
    def _():
        pl.semaphore_signal(barrier, inc=1, device_id=(me, mine + 2), device_id_type=mesh_id)

    pl.semaphore_signal(barrier, inc=1, device_id=peers[2], device_id_type=mesh_id)
    for d in range(1, 4):
        pl.semaphore_signal(barrier, inc=1, device_id=(lax.rem(me + d, 4), mine), device_id_type=mesh_id)
    own = [
        pltpu.make_async_copy(panel_ref.at[pl.ds(h * half, half)], buf.at[mine * PIECES + h], own_sem.at[h])
        for h in range(PIECES)
    ]
    for c in own:
        c.start()
    my_rows = pl.ds(pl.multiple_of(me * part, 8), part)
    s_ref[my_rows, :] = diag_ref[...]
    for c in own:
        c.wait()
    pl.semaphore_wait(barrier, 4 + jnp.where(z > 0, 1, 0) + jnp.where(z < 3, 1, 0))

    copies = []
    for d in range(1, 4):
        copies.append(
            pltpu.make_async_remote_copy(
                src_ref=s_ref.at[my_rows],
                dst_ref=s_ref.at[my_rows],
                send_sem=diag_send.at[d - 1],
                recv_sem=diag_recv.at[d - 1],
                device_id=(lax.rem(me + d, 4), mine),
                device_id_type=mesh_id,
            )
        )
        copies[-1].start()

    def pick(values):
        packed = [sum(values.get((r, c), NONE) * BASE**r for r in range(4)) for c in range(8)]
        got = jnp.int32(packed[7])
        for c in range(7):
            got = jnp.where(mine == c, packed[c], got)
        return got

    def digit(packed):
        got = lax.rem(packed, BASE)
        for r in range(1, 4):
            got = jnp.where(me == r, lax.rem(lax.div(packed, BASE**r), BASE), got)
        return got

    def look(t, way, side):
        if isinstance(t, int):
            values = table[t][way][side]
            return digit(pick(values)) if values else None
        got = pick(table[LAG][way][side])
        for i in range(LAG + 1, min(slots, size // B * TICKS + LAG)):
            got = jnp.where(t == i, pick(table[i][way][side]), got)
        return digit(got)

    def copy(way, t, place):
        if way >= 3:
            src = jnp.where(me == z, place - 8 * PIECES + 4 * PIECES * y, place)
        else:
            src = place
        return pltpu.make_async_remote_copy(
            src_ref=buf.at[src],
            dst_ref=buf.at[place],
            send_sem=send_sem.at[t % DEPTH if isinstance(t, int) else lax.rem(t, DEPTH), way],
            recv_sem=recv_sem.at[place],
            device_id=peers[way],
            device_id_type=mesh_id,
        )

    def tick(t, before):
        now = []
        for way in range(5):
            done = before[0][way] if len(before) == DEPTH else None
            if done is not None:

                @pl.when(done < NONE)
                def _(way=way, done=done):
                    copy(way, t, done).wait_send()

            if isinstance(t, int) and t >= slots:
                now.append(None)
                continue
            send, first = look(t, way, 0), look(t, way, 1)
            if first is not None:

                @pl.when(first < NONE)
                def _(first=first):
                    copy(0, 0, first).wait_recv()

            if send is not None:

                @pl.when(send < NONE)
                def _(way=way, send=send):
                    copy(way, t, send).start()

            now.append(send)
        return (before + [now])[-DEPTH:]

    before = []
    for i in range(LAG):
        before = tick(i, before)
    row = lax.broadcasted_iota(jnp.int32, (size, size), 0)
    lane = lax.broadcasted_iota(jnp.int32, (size, size), 1)
    x_ref[...] = jnp.where(row == lane, 1.0, 0.0).astype(F32)
    for c in copies:
        c.wait()
    none = jnp.int32(NONE)
    before = [[none] * 5] * (DEPTH - LAG) + before

    def flat(before):
        return tuple(none if v is None else v for now in before for v in now)

    def deep(carry):
        return [list(carry[5 * i : 5 * i + 5]) for i in range(DEPTH)]

    def block(b, carry):
        o = pl.multiple_of(b * B, B)
        here = pl.ds(o, B)
        before = tick(b * TICKS + LAG, deep(carry))
        upper, inv = eliminate(s_ref.at[here, here])
        for i in range(1, TICKS):
            before = tick(b * TICKS + LAG + i, before)
        below = lax.broadcasted_iota(jnp.int32, (size, B), 0) >= o + B
        panel = jnp.where(below, dot(s_ref[:, here], inv, ((1,), (1,))), 0.0)
        l_ref[:, here] = panel
        l_ref[here, here] = upper.T
        x = dot(inv, x_ref[here, :])
        s_ref[...] = s_ref[...] - dot(panel, panel, ((1,), (1,)))
        x_ref[...] = x_ref[...] - dot(panel, x)
        x_ref[here, :] = x
        return flat(before)

    before = deep(lax.fori_loop(0, size // B, block, flat(before)))
    t = size // B * TICKS + LAG
    before = tick(t, before)
    l_own[...] = l_ref[my_rows, :]
    x = x_ref[...]
    t = t + 1
    cut = panel_ref.shape[0] // 2
    for i in range(2):
        rows = slice(i * cut, (i + 1) * cut)
        f_ref[rows, :] = dot(panel_ref[rows, :], x, ((1,), (1,)))
        before = tick(t, before)
        t = t + 1
    cut = B * (size // B // 2)
    for rows in (slice(0, cut), slice(cut, size)):
        si_ref[rows, :] = dot(x[:, rows], x, ((0,), (0,)))
        before = tick(t, before)
        t = t + 1
    for i in range(t, slots + DEPTH):
        before = tick(i, before)
    for first in range(0, buf.shape[0], 6):
        some = {d: sum((p in places) << (p - first) for p in range(first, first + 6)) for d, places in rest.items()}
        bits = digit(pick(some))
        for p in range(first, min(first + 6, buf.shape[0])):

            @pl.when(lax.rem(lax.div(bits, 2 ** (p - first)), 2) == 1)
            def _(p=p):
                copy(0, 0, p).wait_recv()


def exchange(diag_block, panel, n_col):
    size = diag_block.shape[1]
    rows = panel.shape[0]
    table, rest = tables(make_plan(SEED))
    places = (n_col + n_col // 2) * PIECES
    dma = pltpu.SemaphoreType.DMA
    return pl.pallas_call(
        functools.partial(exchange_kernel, table, rest),
        out_shape=[
            jax.ShapeDtypeStruct((places, rows // PIECES, size), F32),
            jax.ShapeDtypeStruct(diag_block.shape, F32),
            jax.ShapeDtypeStruct(panel.shape, F32),
            jax.ShapeDtypeStruct((size, size), F32),
        ],
        in_specs=[VMEM, VMEM],
        out_specs=[pl.BlockSpec(memory_space=pl.ANY), VMEM, VMEM, VMEM],
        scratch_shapes=[pltpu.VMEM((size, size), F32)] * 3
        + [dma((DEPTH, 5)), dma((places,)), dma((PIECES,)), dma((3,)), dma((3,))],
        compiler_params=pltpu.CompilerParams(collective_id=0, has_side_effects=True, vmem_limit_bytes=50 << 20),
        cost_estimate=cost(14e9, 4 * rows * size * 12),
        name="exchange",
    )(diag_block, panel)


def gather_plain(panel, n_row, n_col):
    rows = panel.shape[0]
    me, mine = lax.axis_index("prow"), lax.axis_index("pcol")
    row_panel = lax.all_gather(panel, "pcol", axis=0, tiled=True)
    owner = mine * n_row // n_col
    start = mine * n_row * rows - owner * n_col * rows
    block = lax.dynamic_slice_in_dim(row_panel, start, n_row * rows, 0)
    return row_panel, lax.psum(jnp.where(me == owner, block, 0.0), "prow")


def local(n_row, n_col, diag_block, panel_below, trailing):
    if (n_row, n_col) == (4, 8):
        buf, factor_diag, own, inverse = exchange(diag_block, panel_below, n_col)
        blocks = buf.reshape((-1, buf.shape[2]))
        z, y = lax.axis_index("pcol") // 2, lax.axis_index("pcol") % 2
        where = jnp.where(lax.axis_index("prow") == z, y, 2).astype(jnp.int32)
        return factor_diag, own, update(inverse, blocks, blocks, trailing, where)
    whole_diag = gather_diag(diag_block, n_row)
    rows, columns = gather_plain(panel_below, n_row, n_col)
    factor, inverse, own = factorize(whole_diag, panel_below)
    diag_rows = diag_block.shape[0]
    factor_diag = lax.dynamic_slice_in_dim(factor, lax.axis_index("prow") * diag_rows, diag_rows, 0)
    return factor_diag, own, update(inverse, columns, rows, trailing)


def solution(mesh):
    return jax.shard_map(
        functools.partial(local, mesh.shape["prow"], mesh.shape["pcol"]),
        mesh=mesh,
        in_specs=(P("prow", None), P(("prow", "pcol"), None), P("prow", "pcol")),
        out_specs=(P("prow", None), P(("prow", "pcol"), None), P("prow", "pcol")),
        check_vma=False,
    )
```

```python
import functools
import random

import jax
import jax.numpy as jnp
import numpy as np
from jax import lax
from jax.experimental import pallas as pl
from jax.experimental.pallas import tpu as pltpu
from jax.sharding import PartitionSpec as P

B = 128
F32 = jnp.float32
BF16 = jnp.bfloat16
VMEM = pl.BlockSpec(memory_space=pltpu.VMEM)


def dot(a, b, contract=((1,), (0,)), precision=lax.Precision.HIGHEST):
    return lax.dot_general(a, b, (contract, ((), ())), precision=precision, preferred_element_type=F32)


def split(x):
    high = x.astype(BF16)
    return high, (x - high.astype(F32)).astype(BF16)


def lanes(x, q):
    return jnp.broadcast_to(x[:, q : q + 1], (8, B))


def sublanes(x, i):
    return jnp.broadcast_to(x[i : i + 1, :], (8, B))


def eliminate(block_ref):
    count = B // 8
    sub = lax.broadcasted_iota(jnp.int32, (8, B), 0)
    lane = lax.broadcasted_iota(jnp.int32, (8, B), 1)
    a = [block_ref[8 * r : 8 * r + 8, :B] for r in range(count)]
    m = [jnp.where(lane == sub + 8 * r, 1.0, 0.0).astype(F32) for r in range(count)]
    upper, inv = [], []
    for g in range(count):
        columns = [lanes(a[g], 8 * g + q) for q in range(8)]
        d = {(i, q): sublanes(columns[q], i) for q in range(8) for i in range(q + 1)}
        ua = [sublanes(a[g], q) for q in range(8)]
        um = [sublanes(m[g], q) for q in range(8)]
        scale = []
        for p in range(8):
            scale.append(lax.rsqrt(d[p, p]))
            for q in range(p + 1, 8):
                d[p, q] = d[p, q] * scale[p]
            ua[p] = ua[p] * scale[p]
            um[p] = um[p] * scale[p]
            for i in range(p + 1, 8):
                for q in range(i, 8):
                    d[i, q] = d[i, q] - d[p, i] * d[p, q]
                ua[i] = ua[i] - d[p, i] * ua[p]
                um[i] = um[i] - d[p, i] * um[p]
        rows_a, rows_m = ua[7], um[7]
        for q in range(7):
            rows_a = jnp.where(sub == q, ua[q], rows_a)
            rows_m = jnp.where(sub == q, um[q], rows_m)
        upper.append(jnp.where(lane >= sub + 8 * g, rows_a, 0.0))
        inv.append(rows_m)
        if g == count - 1:
            break
        for p in range(7, -1, -1):
            ua[p] = ua[p] * scale[p]
            um[p] = um[p] * scale[p]
            for q in range(p):
                ua[q] = ua[q] - d[q, p] * ua[p]
                um[q] = um[q] - d[q, p] * um[p]
        for r in range(g + 1, count):
            column = lanes(a[r], 8 * g)
            sum_a, sum_m = column * ua[0], column * um[0]
            for q in range(1, 8):
                column = lanes(a[r], 8 * g + q)
                sum_a = sum_a + column * ua[q]
                sum_m = sum_m + column * um[q]
            a[r] = a[r] - sum_a
            m[r] = m[r] - sum_m
    return jnp.concatenate(upper, 0), jnp.concatenate(inv, 0)


def step_kernel(k, rest, *refs):
    s_ref = refs[0]
    refs = refs[1:]
    t_ref = None
    if k:
        t_ref, refs = refs[0], refs[1:]
    l_ref, x_ref = refs[0], refs[1]
    upper, inv = eliminate(s_ref)
    l_ref[:B, :] = upper.T
    if k:
        x_ref[:, : B * k] = dot(inv, t_ref[:B, :])
    x_ref[:, B * k :] = inv
    if rest:
        panel = dot(s_ref[B:, :B], inv, ((1,), (1,)))
        l_ref[B:, :] = panel
        s_out, t_out = refs[2], refs[3]
        s_out[...] = s_ref[B:, B:] - dot(panel, panel, ((1,), (1,)))
        if k:
            t_out[:, : B * k] = t_ref[B:, :] - dot(panel, x_ref[:, : B * k])
        t_out[:, B * k :] = -dot(panel, inv)


def finish_kernel(nb, *refs):
    ls, xs, panel_ref = refs[:nb], refs[nb : 2 * nb], refs[2 * nb]
    l_ref, si_ref, f_ref, x_ref = refs[2 * nb + 1 :]
    l_ref[...] = jnp.zeros_like(l_ref)
    x_ref[...] = jnp.zeros_like(x_ref)
    for k in range(nb):
        l_ref[B * k :, B * k : B * k + B] = ls[k][...]
        x_ref[B * k : B * k + B, : B * k + B] = xs[k][...]
    x = x_ref[...]
    f_ref[...] = dot(panel_ref[...], x, ((1,), (1,)))
    si_ref[...] = dot(x, x, ((0,), (0,)))


def cost(flops, size):
    return pl.CostEstimate(flops=int(flops), bytes_accessed=int(size), transcendentals=0)


PARAMS = dict(vmem_limit_bytes=40 << 20)


def factorize(whole_diag, panel):
    size = whole_diag.shape[0]
    nb = size // B
    s, t = whole_diag, None
    ls, xs = [], []
    for k in range(nb):
        n = size - B * k
        rest = n - B
        out = [jax.ShapeDtypeStruct((n, B), F32), jax.ShapeDtypeStruct((B, B * (k + 1)), F32)]
        if rest:
            out += [jax.ShapeDtypeStruct((rest, rest), F32), jax.ShapeDtypeStruct((rest, B * (k + 1)), F32)]
        args = [s] + ([t] if k else [])
        res = pl.pallas_call(
            functools.partial(step_kernel, k, rest),
            out_shape=out,
            in_specs=[VMEM] * len(args),
            out_specs=[VMEM] * len(out),
            compiler_params=pltpu.CompilerParams(**PARAMS),
            cost_estimate=cost(14e9, 4 * n * n),
            name="diag_step",
        )(*args)
        ls.append(res[0])
        xs.append(res[1])
        if rest:
            s, t = res[2], res[3]
    return pl.pallas_call(
        functools.partial(finish_kernel, nb),
        out_shape=[
            jax.ShapeDtypeStruct((size, size), F32),
            jax.ShapeDtypeStruct((size, size), F32),
            jax.ShapeDtypeStruct(panel.shape, F32),
        ],
        in_specs=[VMEM] * (2 * nb + 1),
        out_specs=[VMEM] * 3,
        scratch_shapes=[pltpu.VMEM((size, size), F32)],
        compiler_params=pltpu.CompilerParams(**PARAMS),
        cost_estimate=cost(8e9, 4 * 5 * size * size),
        name="diag_finish",
    )(*ls, *xs, panel)


def update_kernel(where_ref, si_ref, col_ref, row_ref, t_ref, o_ref, w_ref):
    k = si_ref.shape[0]

    @pl.when(pl.program_id(0) == 0)
    def _():
        high, low = split(si_ref[...])
        left = jnp.concatenate([high, high, low], 1)
        width = w_ref.shape[1]
        tile = 256 if width % 256 == 0 else width
        for c in range(0, width, tile):
            bh, bl = split(col_ref[c : c + tile, :])
            right = jnp.concatenate([bh, bl, bh], 1)
            w = dot(left, right, ((1,), (1,)), lax.Precision.DEFAULT)
            wh, wl = split(w)
            w_ref[:k, c : c + tile] = wh
            w_ref[k : 2 * k, c : c + tile] = wl
            w_ref[2 * k :, c : c + tile] = wh

    high, low = split(row_ref[...])
    a = jnp.concatenate([high, high, low], 1)
    o_ref[...] = t_ref[...] - dot(a, w_ref[...], precision=lax.Precision.DEFAULT)


def update(inverse, columns, rows, trailing, where=None):
    m, n = trailing.shape
    k = inverse.shape[0]
    tm = next(s for s in (384, 256, 128, 64, 32, 16, 8) if m % s == 0)
    where = jnp.zeros((1,), jnp.int32) if where is None else where.reshape((1,))
    return pl.pallas_call(
        update_kernel,
        grid_spec=pltpu.PrefetchScalarGridSpec(
            num_scalar_prefetch=1,
            grid=(m // tm,),
            in_specs=[
                pl.BlockSpec((k, k), lambda i, w: (0, 0)),
                pl.BlockSpec((n, k), lambda i, w: (w[0], 0), pipeline_mode=pl.Buffered(1)),
                pl.BlockSpec((tm, k), lambda i, w: (i, 0)),
                pl.BlockSpec((tm, n), lambda i, w: (i, 0)),
            ],
            out_specs=pl.BlockSpec((tm, n), lambda i, w: (i, 0)),
            scratch_shapes=[pltpu.VMEM((3 * k, n), BF16)],
        ),
        out_shape=jax.ShapeDtypeStruct((m, n), F32),
        compiler_params=pltpu.CompilerParams(vmem_limit_bytes=58 << 20),
        cost_estimate=cost(6 * m * n * k, 8 * m * n),
        name="trailing_update",
    )(where, inverse, columns, rows, trailing)


def gather_diag(diag_block, n_row):
    rows = diag_block.shape[0]
    me = lax.axis_index("prow")
    whole = jnp.zeros((rows * n_row, diag_block.shape[1]), F32)
    whole = lax.dynamic_update_slice_in_dim(whole, diag_block, me * rows, 0)
    for d in range(1, n_row):
        got = lax.ppermute(diag_block, "prow", [(i, (i + d) % n_row) for i in range(n_row)])
        whole = lax.dynamic_update_slice_in_dim(whole, got, (me + n_row - d) % n_row * rows, 0)
    return whole


PIECES = 4
LAG = 3
DEPTH = 5
SEED = 2
BASE = 64
NONE = BASE - 1
TICKS = 3


def peer_of(device, way):
    r, c = device
    if way == 0:
        return (r, c - 2) if c >= 2 else None
    if way == 1:
        return (r, c + 2) if c < 6 else None
    return ((r, c ^ 1), (r ^ 2, c), (r ^ 1, c))[way - 2]


def make_plan(seed):
    draw = random.Random(seed)
    devices = [(r, c) for r in range(4) for c in range(8)]
    column_of = lambda b: 2 * b[0] + b[1] // 4
    far = lambda d, e: abs(d[1] // 2 - e[1] // 2) + abs(d[1] % 2 - e[1] % 2)
    every = [(r, c, h) for r in range(4) for c in range(8) for h in range(PIECES)]
    need = {d: {b for b in every if b[0] == d[0] or column_of(b) == d[1]} for d in devices}
    got = {d: {(*d, h): 0 for h in range(PIECES)} for d in devices}
    plan = []
    while not all(need[d] <= set(got[d]) for d in devices):
        t, slot = len(plan), {}

        def choose(senders, way, score):
            best = None
            for d in senders:
                e = peer_of(d, way)
                for b, ready in got[d].items():
                    if e is None or ready > t or b in got[e] or b not in need[e]:
                        continue
                    s = score(d, e, b, ready)
                    if s is not None and (best is None or s > best[0]):
                        best = s, d, e, b
            if best:
                slot[best[1], way] = best[3]
                got[best[2]][best[3]] = t + LAG

        def row_score(d, e, b, ready):
            home = (b[0], column_of(b))
            near = min(far((b[0], o), home) for o in range(8) if b in got[b[0], o])
            urgent = b not in got[home] and far(e, home) < far(d, home) == near
            lack = sum(b not in got[b[0], o] for o in range(8))
            return urgent, far(d, home) if urgent else lack, draw.random()

        def column_score(d, e, b, ready):
            return (-ready, draw.random()) if column_of(b) == d[1] and e[0] != b[0] else None

        links = [(x, c, way) for x in range(2) for c in range(8) for way in range(3)]
        draw.shuffle(links)
        for x, c, way in links:
            choose([(2 * x, c), (2 * x + 1, c)], way, row_score)
        for x in range(2):
            for c in range(8):
                choose([(2 * x, c), (2 * x + 1, c)], 3, lambda d, e, b, ready: column_score(d, e, b, ready) if b[0] == d[0] else None)
        for d in devices:
            choose([d], 4, column_score)
        plan.append(slot)
    return plan


def place_of(device, b):
    r, c, h = b
    return c * PIECES + h if r == device[0] else 8 * PIECES + c % 4 * PIECES + h


def tables(plan):
    out, rest = [], {}
    waited = {(r, c): {(r, c, h) for h in range(PIECES)} for r in range(4) for c in range(8)}
    for slot in plan:
        ways = []
        for way in range(5):
            send, first = {}, {}
            for (d, w), b in slot.items():
                if w == way:
                    e = peer_of(d, way)
                    send[d] = place_of(e, b)
                    rest.setdefault(e, []).append(b)
            ways.append((send, first))
        for way in range(5):
            for (d, w), b in slot.items():
                if w == way and b not in waited[d]:
                    ways[way][1][d] = place_of(d, b)
                    waited[d].add(b)
        out.append(ways)
    rest = {d: [place_of(d, b) for b in got if b not in waited[d]] for d, got in rest.items()}
    return out, rest


def exchange_kernel(table, rest, diag_ref, panel_ref, buf, l_own, f_ref, si_ref, s_ref, l_ref, x_ref, send_sem, recv_sem, own_sem, diag_send, diag_recv):
    slots = len(table)
    me, mine = lax.axis_index("prow"), lax.axis_index("pcol")
    z, y = lax.div(mine, 2), lax.rem(mine, 2)
    size = s_ref.shape[0]
    part = diag_ref.shape[0]
    half = buf.shape[1]
    other = lax.rem(me + 2, 4)
    sibling = me + 1 - 2 * lax.rem(me, 2)
    peers = [(me, mine - 2), (me, mine + 2), (me, mine + 1 - 2 * y), (other, mine), (sibling, mine)]
    mesh_id = pl.DeviceIdType.MESH

    barrier = pltpu.get_barrier_semaphore()

    @pl.when(z > 0)
    def _():
        pl.semaphore_signal(barrier, inc=1, device_id=(me, mine - 2), device_id_type=mesh_id)

    @pl.when(z < 3)
    def _():
        pl.semaphore_signal(barrier, inc=1, device_id=(me, mine + 2), device_id_type=mesh_id)

    pl.semaphore_signal(barrier, inc=1, device_id=peers[2], device_id_type=mesh_id)
    for d in range(1, 4):
        pl.semaphore_signal(barrier, inc=1, device_id=(lax.rem(me + d, 4), mine), device_id_type=mesh_id)
    own = [
        pltpu.make_async_copy(panel_ref.at[pl.ds(h * half, half)], buf.at[mine * PIECES + h], own_sem.at[h])
        for h in range(PIECES)
    ]
    for c in own:
        c.start()
    my_rows = pl.ds(pl.multiple_of(me * part, 8), part)
    s_ref[my_rows, :] = diag_ref[...]
    for c in own:
        c.wait()
    pl.semaphore_wait(barrier, 4 + jnp.where(z > 0, 1, 0) + jnp.where(z < 3, 1, 0))

    copies = []
    for d in range(1, 4):
        copies.append(
            pltpu.make_async_remote_copy(
                src_ref=s_ref.at[my_rows],
                dst_ref=s_ref.at[my_rows],
                send_sem=diag_send.at[d - 1],
                recv_sem=diag_recv.at[d - 1],
                device_id=(lax.rem(me + d, 4), mine),
                device_id_type=mesh_id,
            )
        )
        copies[-1].start()

    def pick(values):
        packed = [sum(values.get((r, c), NONE) * BASE**r for r in range(4)) for c in range(8)]
        got = jnp.int32(packed[7])
        for c in range(7):
            got = jnp.where(mine == c, packed[c], got)
        return got

    def digit(packed):
        got = lax.rem(packed, BASE)
        for r in range(1, 4):
            got = jnp.where(me == r, lax.rem(lax.div(packed, BASE**r), BASE), got)
        return got

    def look(t, way, side):
        if isinstance(t, int):
            values = table[t][way][side]
            return digit(pick(values)) if values else None
        got = pick(table[LAG][way][side])
        for i in range(LAG + 1, min(slots, size // B * TICKS + LAG)):
            got = jnp.where(t == i, pick(table[i][way][side]), got)
        return digit(got)

    def copy(way, t, place):
        if way >= 3:
            src = jnp.where(me == z, place - 8 * PIECES + 4 * PIECES * y, place)
        else:
            src = place
        return pltpu.make_async_remote_copy(
            src_ref=buf.at[src],
            dst_ref=buf.at[place],
            send_sem=send_sem.at[t % DEPTH if isinstance(t, int) else lax.rem(t, DEPTH), way],
            recv_sem=recv_sem.at[place],
            device_id=peers[way],
            device_id_type=mesh_id,
        )

    def tick(t, before):
        now = []
        for way in range(5):
            done = before[0][way] if len(before) == DEPTH else None
            if done is not None:

                @pl.when(done < NONE)
                def _(way=way, done=done):
                    copy(way, t, done).wait_send()

            if isinstance(t, int) and t >= slots:
                now.append(None)
                continue
            send, first = look(t, way, 0), look(t, way, 1)
            if first is not None:

                @pl.when(first < NONE)
                def _(first=first):
                    copy(0, 0, first).wait_recv()

            if send is not None:

                @pl.when(send < NONE)
                def _(way=way, send=send):
                    copy(way, t, send).start()

            now.append(send)
        return (before + [now])[-DEPTH:]

    before = []
    for i in range(LAG):
        before = tick(i, before)
    row = lax.broadcasted_iota(jnp.int32, (size, size), 0)
    lane = lax.broadcasted_iota(jnp.int32, (size, size), 1)
    x_ref[...] = jnp.where(row == lane, 1.0, 0.0).astype(F32)
    for c in copies:
        c.wait()
    none = jnp.int32(NONE)
    before = [[none] * 5] * (DEPTH - LAG) + before

    def flat(before):
        return tuple(none if v is None else v for now in before for v in now)

    def deep(carry):
        return [list(carry[5 * i : 5 * i + 5]) for i in range(DEPTH)]

    def block(b, carry):
        o = pl.multiple_of(b * B, B)
        here = pl.ds(o, B)
        before = tick(b * TICKS + LAG, deep(carry))
        upper, inv = eliminate(s_ref.at[here, here])
        for i in range(1, TICKS):
            before = tick(b * TICKS + LAG + i, before)
        below = lax.broadcasted_iota(jnp.int32, (size, B), 0) >= o + B
        panel = jnp.where(below, dot(s_ref[:, here], inv, ((1,), (1,))), 0.0)
        l_ref[:, here] = panel
        l_ref[here, here] = upper.T
        x = dot(inv, x_ref[here, :])
        s_ref[...] = s_ref[...] - dot(panel, panel, ((1,), (1,)))
        x_ref[...] = x_ref[...] - dot(panel, x)
        x_ref[here, :] = x
        return flat(before)

    before = deep(lax.fori_loop(0, size // B, block, flat(before)))
    t = size // B * TICKS + LAG
    before = tick(t, before)
    l_own[...] = l_ref[my_rows, :]
    x = x_ref[...]
    t = t + 1
    cut = panel_ref.shape[0] // 2
    for i in range(2):
        rows = slice(i * cut, (i + 1) * cut)
        f_ref[rows, :] = dot(panel_ref[rows, :], x, ((1,), (1,)))
        before = tick(t, before)
        t = t + 1
    cut = B * (size // B // 2)
    for rows in (slice(0, cut), slice(cut, size)):
        si_ref[rows, :] = dot(x[:, rows], x, ((0,), (0,)))
        before = tick(t, before)
        t = t + 1
    for i in range(t, slots + DEPTH):
        before = tick(i, before)
    for first in range(0, buf.shape[0], 6):
        some = {d: sum((p in places) << (p - first) for p in range(first, first + 6)) for d, places in rest.items()}
        bits = digit(pick(some))
        for p in range(first, min(first + 6, buf.shape[0])):

            @pl.when(lax.rem(lax.div(bits, 2 ** (p - first)), 2) == 1)
            def _(p=p):
                copy(0, 0, p).wait_recv()


def exchange(diag_block, panel, n_col):
    size = diag_block.shape[1]
    rows = panel.shape[0]
    table, rest = tables(make_plan(SEED))
    places = (n_col + n_col // 2) * PIECES
    dma = pltpu.SemaphoreType.DMA
    return pl.pallas_call(
        functools.partial(exchange_kernel, table, rest),
        out_shape=[
            jax.ShapeDtypeStruct((places, rows // PIECES, size), F32),
            jax.ShapeDtypeStruct(diag_block.shape, F32),
            jax.ShapeDtypeStruct(panel.shape, F32),
            jax.ShapeDtypeStruct((size, size), F32),
        ],
        in_specs=[VMEM, VMEM],
        out_specs=[pl.BlockSpec(memory_space=pl.ANY), VMEM, VMEM, VMEM],
        scratch_shapes=[pltpu.VMEM((size, size), F32)] * 3
        + [dma((DEPTH, 5)), dma((places,)), dma((PIECES,)), dma((3,)), dma((3,))],
        compiler_params=pltpu.CompilerParams(collective_id=0, has_side_effects=True, vmem_limit_bytes=50 << 20),
        cost_estimate=cost(14e9, 4 * rows * size * 12),
        name="exchange",
    )(diag_block, panel)


def gather_plain(panel, n_row, n_col):
    rows = panel.shape[0]
    me, mine = lax.axis_index("prow"), lax.axis_index("pcol")
    row_panel = lax.all_gather(panel, "pcol", axis=0, tiled=True)
    owner = mine * n_row // n_col
    start = mine * n_row * rows - owner * n_col * rows
    block = lax.dynamic_slice_in_dim(row_panel, start, n_row * rows, 0)
    return row_panel, lax.psum(jnp.where(me == owner, block, 0.0), "prow")


def local(n_row, n_col, diag_block, panel_below, trailing):
    if (n_row, n_col) == (4, 8):
        buf, factor_diag, own, inverse = exchange(diag_block, panel_below, n_col)
        blocks = buf.reshape((-1, buf.shape[2]))
        z, y = lax.axis_index("pcol") // 2, lax.axis_index("pcol") % 2
        where = jnp.where(lax.axis_index("prow") == z, y, 2).astype(jnp.int32)
        return factor_diag, own, update(inverse, blocks, blocks, trailing, where)
    whole_diag = gather_diag(diag_block, n_row)
    rows, columns = gather_plain(panel_below, n_row, n_col)
    factor, inverse, own = factorize(whole_diag, panel_below)
    diag_rows = diag_block.shape[0]
    factor_diag = lax.dynamic_slice_in_dim(factor, lax.axis_index("prow") * diag_rows, diag_rows, 0)
    return factor_diag, own, update(inverse, columns, rows, trailing)


def solution(mesh):
    return jax.shard_map(
        functools.partial(local, mesh.shape["prow"], mesh.shape["pcol"]),
        mesh=mesh,
        in_specs=(P("prow", None), P(("prow", "pcol"), None), P("prow", "pcol")),
        out_specs=(P("prow", None), P(("prow", "pcol"), None), P("prow", "pcol")),
        check_vma=False,
    )
```
